32 devices in a mesh: leaf: 2 (over x), rows: 16 (over z, y, core).
Axes of the slice: x: 2, y: 2, z: 4, core: 2. Of those that a mesh axis runs over, the one named last changes fastest.
Arguments:
- features: bfloat16 [262144, 256], P(('leaf', 'rows')), parts along dimension 0, may hold values from -80 to 80
- node_ids: int32 [262144], P(('leaf', 'rows')), parts along dimension 0, may hold values from -1 to 15, as said below
- labels: int32 [262144], P(('leaf', 'rows')), parts along dimension 0, may hold values from 0 to 15
- owners: int32 [32], P('leaf'), parts along dimension 0, may hold values from 0 to 15, each once
Outputs:
- hyperplanes: float32 [32, 16, 256], P(('leaf', 'rows')), parts along dimension 0
- scores: float32 [16, 262144], P(None, ('leaf', 'rows')), parts along dimension 1
The draws below stay inside these ranges and needn't reach their ends.
There are 2 independent parts, one for each index of `leaf`. The reference program is written for one: setup_inputs(seed, part) draws one part's arguments, and reference() takes and returns one part's arrays. A program takes and returns all parts, laid end to end along the dimension named above; each array names one. Nothing has to cross between parts.
Inputs may be any that keep to these rules, and one draw needn't show every extreme that they name: `node_ids`: on rows device d, row p of node n's segment (local row n * 512 + p) holds n or -1; the live rows of a segment come first and there is at least one; some segment of every device is full. Each node number appears once in owners; node n is owned by the device of rows with index owners[n].
All inputs are finite; a program needn't handle non-finite values.
Results may differ from the reference program's by a relative error of at most 0.0035.
Values may be sent and summed in bfloat16 or wider, within the bound.
A program may use at most 128 MiB of HBM per device.

```python
import math
import jax
import jax.numpy as jnp
from jax import lax

F = 256
CLASSES = 16
ROW_DEV = 8192
NODES = 16
SEG = 512
TOTAL_ROWS = 131072
N_ROWS = 16


def label_draw(key):
    positions = jnp.arange(TOTAL_ROWS, dtype=jnp.int32)
    node_of = positions % ROW_DEV // SEG
    present = jax.random.randint(jax.random.fold_in(key, 11), (NODES, CLASSES), 0, 4) > 0
    forced = jnp.arange(CLASSES, dtype=jnp.int32)[None, :] == (jnp.arange(NODES, dtype=jnp.int32) % CLASSES)[:, None]
    present = (present | forced).astype(jnp.int32)
    noise = jax.random.randint(jax.random.fold_in(key, 12), (TOTAL_ROWS, CLASSES), 0, 1 << 20)
    ranked = noise + present[node_of] * (1 << 21)
    return jnp.argmax(ranked, axis=1).astype(jnp.int32)


def draw_labels(key, part):
    return label_draw(jax.random.fold_in(key, 5))


def draw_features(key, part):
    marks = label_draw(jax.random.fold_in(key, 5))
    base = jax.random.normal(jax.random.fold_in(key, 21), (TOTAL_ROWS, F), jnp.float32)
    mixing = jnp.eye(F, dtype=jnp.float32) + 0.5 * jax.random.normal(jax.random.fold_in(key, 22), (F, F), jnp.float32) / math.sqrt(F)
    centres = jax.random.normal(jax.random.fold_in(key, 23), (CLASSES, F), jnp.float32)
    values = jnp.dot(base, mixing, precision=lax.Precision.HIGHEST) + centres[marks]
    return jnp.clip(values, -80.0, 80.0).astype(jnp.bfloat16)


def draw_node_ids(key, part):
    device = jnp.arange(N_ROWS, dtype=jnp.int32)
    ceiling = jnp.maximum((SEG + 2 * SEG * device // max(N_ROWS - 1, 1)) // 3, 1)
    lengths = jax.random.randint(jax.random.fold_in(key, 31), (N_ROWS, NODES), 1, ceiling[:, None] + 1)
    filled = jnp.arange(NODES, dtype=jnp.int32)[None, :] == (device % NODES)[:, None]
    lengths = jnp.where(filled, SEG, lengths)
    within = jnp.arange(SEG, dtype=jnp.int32)
    node_index = jnp.broadcast_to(jnp.arange(NODES, dtype=jnp.int32)[None, :, None], (N_ROWS, NODES, SEG))
    result = jnp.where(within[None, None, :] < lengths[:, :, None], node_index, -1)
    return result.reshape(TOTAL_ROWS).astype(jnp.int32)


def setup_inputs(seed: int = 0, part: int = 0) -> dict:
    keys = jax.random.split(jax.random.key(seed), 5)
    own_keys = jax.random.split(jax.random.fold_in(keys[4], part), 5)
    return {
        "features": draw_features(jax.random.fold_in(jax.random.fold_in(keys[4], part), 71), part),
        "node_ids": draw_node_ids(jax.random.fold_in(jax.random.fold_in(keys[4], part), 71), part),
        "labels": draw_labels(jax.random.fold_in(jax.random.fold_in(keys[4], part), 71), part),
        "owners": jax.random.permutation(own_keys[3], NODES).astype(jnp.int32),
    }


ridge_term = 0.1

def solve_nodes(scatter, sums, counts):
    totals = jnp.sum(counts, axis=1)
    centers = jnp.sum(sums, axis=1) / totals[:, None]
    scaled = sums / jnp.maximum(counts, 1.0)[:, :, None]
    within = scatter - jnp.einsum('ncf,ncg->nfg', scaled, sums, precision=lax.Precision.HIGHEST)
    identity = jnp.eye(scatter.shape[-1], dtype=jnp.float32)
    system = within / totals[:, None, None] + ridge_term * identity
    shifts = (sums - counts[:, :, None] * centers[:, None, :]) / totals[:, None, None]
    factor = jnp.linalg.cholesky(system)
    planes = jax.vmap(lambda lower, right: jax.scipy.linalg.cho_solve((lower, True), right.T).T)(factor, shifts)
    offsets = -jnp.einsum('ncf,nf->nc', planes, centers, precision=lax.Precision.HIGHEST)
    return (planes, offsets)

def reference(features, node_ids, labels, owners):
    blocks = features.reshape(N_ROWS, NODES, SEG, F)
    live_rows = node_ids.reshape(N_ROWS, NODES, SEG) == jnp.arange(NODES, dtype=jnp.int32)[None, :, None]
    marks = labels.reshape(N_ROWS, NODES, SEG)
    classes = jnp.arange(CLASSES, dtype=jnp.int32)

    def one_node(index):
        chosen = lax.dynamic_index_in_dim(blocks, index, 1, keepdims=False)
        alive = lax.dynamic_index_in_dim(live_rows, index, 1, keepdims=False).reshape(-1)
        tags = lax.dynamic_index_in_dim(marks, index, 1, keepdims=False).reshape(-1)
        values = jnp.where(alive[:, None], chosen.reshape(-1, F).astype(jnp.float32), 0.0)
        onehot = ((tags[None, :] == classes[:, None]) & alive[None, :]).astype(jnp.float32)
        scatter = jnp.dot(values.T.astype(jnp.float32), values.astype(jnp.float32), preferred_element_type=jnp.float32, precision=lax.Precision.HIGHEST)
        sums = jnp.dot(onehot.astype(jnp.float32), values.astype(jnp.float32), preferred_element_type=jnp.float32, precision=lax.Precision.HIGHEST)
        counts = jnp.sum(onehot, axis=1)
        return (scatter, sums, counts)
    scatter, sums, counts = lax.map(one_node, jnp.arange(NODES, dtype=jnp.int32))
    planes, offsets = solve_nodes(scatter, sums, counts)
    inverse = jnp.zeros((NODES,), jnp.int32).at[owners].set(jnp.arange(NODES, dtype=jnp.int32))
    hyperplanes = jnp.take(planes, inverse, axis=0)
    rounded = lax.optimization_barrier(planes.astype(jnp.bfloat16)).astype(jnp.float32)

    def one_device(pair):
        chosen, alive = pair
        result = jnp.einsum('ncf,nsf->cns', rounded, chosen.astype(jnp.float32), precision=lax.Precision.HIGHEST)
        result = result + offsets.T[:, :, None]
        return jnp.where(alive[None], result, 0.0)
    scores = lax.map(one_device, (blocks, live_rows))
    scores = jnp.transpose(scores, (1, 0, 2, 3)).reshape(CLASSES, TOTAL_ROWS)
    return (hyperplanes, scores)
```

```python
import functools
import jax
import jax.numpy as jnp
from jax import lax
from jax.experimental import pallas as pl
from jax.experimental.pallas import tpu as pltpu
from jax.sharding import PartitionSpec as P

CLASSES = 16
LANES = 128
RIDGE = 0.1
HIGHEST = lax.Precision.HIGHEST
TN = (((0,), (0,)), ((), ()))
NT = (((1,), (1,)), ((), ()))


def iota(shape, dim):
    return lax.broadcasted_iota(jnp.int32, shape, dim)


def partial_kernel(nodes_ref, x_ref, ids_ref, labels_ref, out_ref):
    step = pl.program_id(0)
    node = nodes_ref[step]
    seg, feat = x_ref.shape
    half = feat // 2
    pieces = seg // LANES
    ids = ids_ref[pl.ds(node * pieces, pieces), :]
    tags = labels_ref[pl.ds(node * pieces, pieces), :]
    live = ids == node
    length = jnp.sum(live.astype(jnp.int32))
    x = x_ref[...]
    x = jnp.where(iota((seg, feat), 0) < length, x, jnp.zeros((), x.dtype))
    tags = jnp.where(live, tags, -1)
    hot = jnp.concatenate(
        [tags[q : q + 1, :] == iota((CLASSES, LANES), 0) for q in range(pieces)], axis=1
    )
    hot = hot.astype(jnp.float32).astype(jnp.bfloat16)
    moment = lax.dot_general(x, x, TN, preferred_element_type=jnp.float32)
    sums = jnp.dot(hot, x, preferred_element_type=jnp.float32)
    counts = lax.dot_general(
        jnp.ones((8, seg), jnp.bfloat16), hot, NT, preferred_element_type=jnp.float32
    )
    row, col = iota((half, half), 0), iota((half, half), 1)
    low = moment[half:, half:]
    packed = jnp.where(row >= col, moment[:half, :half], low)
    diag = jnp.sum(jnp.where(row == col, low, 0.0), axis=0, keepdims=True)
    out_ref[0, 0:half, 0:half] = packed
    out_ref[0, 0:half, half:feat] = moment[:half, half:]
    out_ref[0, half : half + CLASSES, :] = sums
    top = half + CLASSES
    out_ref[0, top : top + 8, 0:half] = jnp.concatenate(
        [counts, jnp.zeros((8, half - CLASSES), jnp.float32)], axis=1
    )
    out_ref[0, top : top + 8, half:feat] = jnp.broadcast_to(diag, (8, half))


def partner_of(me, bit):
    width = 1 << bit
    return me + width * (1 - 2 * ((me // width) % 2))


def reduce_kernel(n, part_ref, out_ref, acc, landed, send_sems, recv_sems):
    bits = n.bit_length() - 1
    me = lax.axis_index("rows")
    barrier = pltpu.get_barrier_semaphore()
    for bit in range(bits):
        pl.semaphore_signal(barrier, inc=1, device_id={"rows": partner_of(me, bit)})
    pl.semaphore_wait(barrier, bits)

    def copy_of(step, q):
        half = n >> (step + 1)
        source = part_ref if step == 0 else acc
        return pltpu.make_async_remote_copy(
            src_ref=source.at[q],
            dst_ref=landed.at[q],
            send_sem=send_sems.at[q],
            recv_sem=recv_sems.at[q],
            device_id={"rows": partner_of(me, step)},
        )

    for q in reversed(range(n // 2, n)):
        copy_of(0, q).start()
    for step in range(bits):
        half = n >> (step + 1)
        for q in reversed(range(half)):
            copy_of(step, q + half).wait_recv()
            base = part_ref if step == 0 else acc
            total = base[q] + landed[q + half]
            if step == bits - 1:
                out_ref[...] = total
            else:
                acc[q] = total
                if q >= half // 2:
                    copy_of(step + 1, q).start()
    for step in range(bits):
        half = n >> (step + 1)
        for q in range(half, 2 * half):
            copy_of(step, q).wait_send()


def lane_of(x, lane):
    index = jnp.full(x.shape, lane, jnp.int32)
    return jnp.take_along_axis(x, index, axis=1, mode="promise_in_bounds")


def solve_kernel(sum_ref, planes_ref, message_ref, work):
    half = LANES
    feat = sum_ref.shape[1]
    top = half + CLASSES
    square = sum_ref[0:half, 0:half]
    turned = square.T
    row, col = iota((half, half), 0), iota((half, half), 1)
    diag = sum_ref[top : top + 1, half:feat]
    first = jnp.where(row >= col, square, turned)
    last = jnp.where(row < col, square, jnp.where(row == col, diag, turned))
    cross = sum_ref[0:half, half:feat]
    sums = sum_ref[half:top, :]
    count_row = sum_ref[top : top + 1, 0:CLASSES]
    eye = iota((CLASSES, CLASSES), 0) == iota((CLASSES, CLASSES), 1)
    counts = jnp.sum(jnp.where(eye, count_row, 0.0), axis=1, keepdims=True)
    total = jnp.sum(counts, axis=0, keepdims=True)
    centers = jnp.sum(sums, axis=0, keepdims=True) / total
    scaled = sums / jnp.maximum(counts, 1.0)
    between = lax.dot_general(
        scaled, sums, TN, precision=HIGHEST, preferred_element_type=jnp.float32
    )
    ridge = jnp.where(row == col, RIDGE, 0.0)
    work[0:half, 0:half] = (first - between[:half, :half]) / total + ridge
    work[0:half, half:feat] = (cross - between[:half, half:]) / total
    work[half:feat, 0:half] = (cross.T - between[half:, :half]) / total
    work[half:feat, half:feat] = (last - between[half:, half:]) / total + ridge
    work[feat : feat + CLASSES, :] = (sums - counts * centers) / total

    rows = feat + CLASSES
    lanes = iota((1, LANES), 1)

    def four(group, base, lane, tile, start):
        pivots = work[pl.ds(group, 8), tile * LANES : (tile + 1) * LANES]
        other = work[pl.ds(group, 8), (1 - tile) * LANES : (2 - tile) * LANES]
        spread = [lane_of(pivots, lane + u) for u in range(4)]
        d = [[spread[u][base + t : base + t + 1, :] for u in range(4)] for t in range(4)]
        a, b, c = d[0][0], d[0][1], d[1][1]
        inv = 1.0 / (a * c - b * b)
        p00, p01, p11 = c * inv, -b * inv, a * inv
        q00, q01, q10, q11 = d[0][2], d[0][3], d[1][2], d[1][3]
        t00, t01 = p00 * q00 + p01 * q10, p00 * q01 + p01 * q11
        t10, t11 = p01 * q00 + p11 * q10, p01 * q01 + p11 * q11
        s00 = d[2][2] - (q00 * t00 + q10 * t10)
        s01 = d[2][3] - (q00 * t01 + q10 * t11)
        s11 = d[3][3] - (q01 * t01 + q11 * t11)
        inv = 1.0 / (s00 * s11 - s01 * s01)
        h00, h01, h11 = s11 * inv, -s01 * inv, s00 * inv
        u00, u01 = t00 * h00 + t01 * h01, t00 * h01 + t01 * h11
        u10, u11 = t10 * h00 + t11 * h01, t10 * h01 + t11 * h11
        e00 = p00 + u00 * t00 + u01 * t01
        e01 = p01 + u00 * t10 + u01 * t11
        e11 = p11 + u10 * t10 + u11 * t11
        dinv = [
            [e00, e01, -u00, -u01],
            [e01, e11, -u10, -u11],
            [-u00, -u10, h00, h01],
            [-u01, -u11, h01, h11],
        ]
        inside = (lanes >= lane) & (lanes < lane + 4)
        near = [
            jnp.where(inside, jnp.where(lanes == lane + t, -1.0, 0.0), pivots[base + t : base + t + 1, :])
            for t in range(4)
        ]
        far = [other[base + t : base + t + 1, :] for t in range(4)]
        mix = lambda r, t: (dinv[t][0] * r[0] + dinv[t][1] * r[1]) + (dinv[t][2] * r[2] + dinv[t][3] * r[3])
        wn = [jnp.broadcast_to(mix(near, t), (8, LANES)) for t in range(4)]
        wf = [jnp.broadcast_to(mix(far, t), (8, LANES)) for t in range(4)]
        inside8 = jnp.broadcast_to(inside, (8, LANES))
        for g in range(start, rows, 8):
            x = work[g : g + 8, tile * LANES : (tile + 1) * LANES]
            y = work[g : g + 8, (1 - tile) * LANES : (2 - tile) * LANES]
            k = [lane_of(x, lane + u) for u in range(4)]
            x = jnp.where(inside8, 0.0, x)
            x = x - ((k[0] * wn[0] + k[1] * wn[1]) + (k[2] * wn[2] + k[3] * wn[3]))
            y = y - ((k[0] * wf[0] + k[1] * wf[1]) + (k[2] * wf[2] + k[3] * wf[3]))
            work[g : g + 8, tile * LANES : (tile + 1) * LANES] = x
            work[g : g + 8, (1 - tile) * LANES : (2 - tile) * LANES] = y

    span = 32
    for start in range(0, feat, span):
        tile = start // LANES

        def body(i, carry):
            group = pl.multiple_of(start + 8 * i, 8)
            lane = start % LANES + 8 * i
            four(group, 0, lane, tile, start)
            four(group, 4, lane + 4, tile, start)
            return carry

        lax.fori_loop(0, span // 8, body, 0)

    planes = work[feat : feat + CLASSES, :]
    planes_ref[...] = planes
    offsets = -jnp.sum(planes * centers, axis=1, keepdims=True)
    high = offsets.astype(jnp.bfloat16).astype(jnp.float32)
    middle = (offsets - high).astype(jnp.bfloat16).astype(jnp.float32)
    low = offsets - high - middle
    lane = iota((CLASSES, feat), 1)
    coded = jnp.where(lane < LANES, high, jnp.where(lane < LANES + LANES // 2, middle, low))
    message_ref[0:CLASSES, :] = planes.astype(jnp.bfloat16)
    message_ref[CLASSES : 2 * CLASSES, :] = coded.astype(jnp.bfloat16)


def gather_kernel(n, mine_ref, out_ref, local_sem, send_sems, recv_sems):
    me = lax.axis_index("rows")
    barrier = pltpu.get_barrier_semaphore()
    for shift in range(1, n):
        pl.semaphore_signal(barrier, inc=1, device_id={"rows": lax.rem(me + shift, n)})
    own = pltpu.make_async_copy(mine_ref, out_ref.at[me], local_sem)
    own.start()
    pl.semaphore_wait(barrier, n - 1)

    def copy_of(shift):
        return pltpu.make_async_remote_copy(
            src_ref=mine_ref,
            dst_ref=out_ref.at[me],
            send_sem=send_sems.at[shift],
            recv_sem=recv_sems.at[shift],
            device_id={"rows": lax.rem(me + shift, n)},
        )

    for shift in range(1, n):
        copy_of(shift).start()
    own.wait()
    for shift in range(1, n):
        copy_of(shift).wait()


def score_kernel(owners_ref, x_ref, ids_ref, message_ref, out_ref):
    node = pl.program_id(0)
    seg = x_ref.shape[0]
    pieces = seg // LANES
    planes = message_ref[0, 0:CLASSES, :]
    coded = message_ref[0, CLASSES : 2 * CLASSES, :].astype(jnp.float32)
    quarter = LANES + LANES // 2
    offsets = coded[:, 0:1] + coded[:, LANES : LANES + 1] + coded[:, quarter : quarter + 1]
    scores = lax.dot_general(planes, x_ref[...], NT, preferred_element_type=jnp.float32)
    scores = scores + offsets
    ids = ids_ref[pl.ds(node * pieces, pieces), :]
    for q in range(pieces):
        block = scores[:, q * LANES : (q + 1) * LANES]
        out_ref[:, q * LANES : (q + 1) * LANES] = jnp.where(ids[q : q + 1, :] == node, block, 0.0)


def reverse_bits(value, bits):
    return int(format(value, "0%db" % bits)[::-1], 2)


def on_device(features, node_ids, labels, owners):
    row_count, feat = features.shape
    n = owners.shape[0]
    seg = row_count // n
    bits = n.bit_length() - 1
    half = feat // 2
    depth = half + CLASSES + 8
    me = lax.axis_index("rows")
    ids = node_ids.reshape(row_count // LANES, LANES)
    tags = labels.reshape(row_count // LANES, LANES)
    order = iota((n, n), 0)
    flipped = sum(((order >> b) & 1) << (bits - 1 - b) for b in range(bits))
    slot = flipped ^ me
    nodes = jnp.sum(jnp.where(owners[None, :] == slot, iota((n, n), 1), 0), axis=1)

    whole = pl.BlockSpec(memory_space=pltpu.VMEM)
    parts = pl.pallas_call(
        partial_kernel,
        grid_spec=pltpu.PrefetchScalarGridSpec(
            num_scalar_prefetch=1,
            grid=(n,),
            in_specs=[pl.BlockSpec((seg, feat), lambda i, nodes: (nodes[i], 0)), whole, whole],
            out_specs=pl.BlockSpec((1, depth, feat), lambda i, nodes: (i, 0, 0)),
        ),
        out_shape=jax.ShapeDtypeStruct((n, depth, feat), jnp.float32),
        name="partials",
    )(nodes, features, ids, tags)

    summed = pl.pallas_call(
        functools.partial(reduce_kernel, n),
        out_shape=jax.ShapeDtypeStruct((depth, feat), jnp.float32),
        in_specs=[whole],
        out_specs=whole,
        scratch_shapes=[
            pltpu.VMEM((n // 2, depth, feat), jnp.float32),
            pltpu.VMEM((n, depth, feat), jnp.float32),
            pltpu.SemaphoreType.DMA((n,)),
            pltpu.SemaphoreType.DMA((n,)),
        ],
        compiler_params=pltpu.CompilerParams(
            collective_id=0, has_side_effects=True, vmem_limit_bytes=60 << 20
        ),
        name="halving",
    )(parts)

    planes, message = pl.pallas_call(
        solve_kernel,
        out_shape=(
            jax.ShapeDtypeStruct((CLASSES, feat), jnp.float32),
            jax.ShapeDtypeStruct((2 * CLASSES, feat), jnp.bfloat16),
        ),
        in_specs=[whole],
        out_specs=(whole, whole),
        scratch_shapes=[pltpu.VMEM((feat + CLASSES, feat), jnp.float32)],
        name="solve",
    )(summed)

    messages = pl.pallas_call(
        functools.partial(gather_kernel, n),
        out_shape=jax.ShapeDtypeStruct((n, 2 * CLASSES, feat), jnp.bfloat16),
        in_specs=[whole],
        out_specs=whole,
        scratch_shapes=[
            pltpu.SemaphoreType.DMA,
            pltpu.SemaphoreType.DMA((n,)),
            pltpu.SemaphoreType.DMA((n,)),
        ],
        compiler_params=pltpu.CompilerParams(collective_id=1, has_side_effects=True),
        name="spread",
    )(message)

    scores = pl.pallas_call(
        score_kernel,
        grid_spec=pltpu.PrefetchScalarGridSpec(
            num_scalar_prefetch=1,
            grid=(n,),
            in_specs=[
                pl.BlockSpec((seg, feat), lambda i, owners: (i, 0)),
                whole,
                pl.BlockSpec((1, 2 * CLASSES, feat), lambda i, owners: (owners[i], 0, 0)),
            ],
            out_specs=pl.BlockSpec((CLASSES, seg), lambda i, owners: (0, i)),
        ),
        out_shape=jax.ShapeDtypeStruct((CLASSES, row_count), jnp.float32),
        name="scores",
    )(owners, features, ids, messages)
    return planes[None], scores


def solution(mesh):
    in_specs = (P(("leaf", "rows"), None), P(("leaf", "rows")), P(("leaf", "rows")), P("leaf"))
    out_specs = (P(("leaf", "rows"), None, None), P(None, ("leaf", "rows")))
    return jax.shard_map(
        on_device, mesh=mesh, in_specs=in_specs, out_specs=out_specs, check_vma=False
    )
```

```python
import functools
import jax
import jax.numpy as jnp
from jax import lax
from jax.experimental import pallas as pl
from jax.experimental.pallas import tpu as pltpu
from jax.sharding import PartitionSpec as P

CLASSES = 16
LANES = 128
RIDGE = 0.1
HIGHEST = lax.Precision.HIGHEST
TN = (((0,), (0,)), ((), ()))
NT = (((1,), (1,)), ((), ()))


def iota(shape, dim):
    return lax.broadcasted_iota(jnp.int32, shape, dim)


def partner_of(me, bit):
    width = 1 << bit
    return me + width * (1 - 2 * ((me // width) % 2))


def one_partial(node, q, x_ref, ids_ref, labels_ref, out_ref):
    seg, feat = x_ref.shape[1:]
    half = feat // 2
    pieces = seg // LANES
    ids = ids_ref[pl.ds(node * pieces, pieces), :]
    tags = labels_ref[pl.ds(node * pieces, pieces), :]
    live = ids == node
    length = jnp.sum(live.astype(jnp.float32), axis=(0, 1), keepdims=True)
    x = x_ref[node]
    position = iota((seg, 1), 0).astype(jnp.float32)
    x = jnp.where(position < length, x, jnp.zeros((), x.dtype))
    tags = jnp.where(live, tags, -1)
    hot = jnp.concatenate(
        [tags[k : k + 1, :] == iota((CLASSES, LANES), 0) for k in range(pieces)], axis=1
    )
    hot = hot.astype(jnp.float32).astype(jnp.bfloat16)
    moment = lax.dot_general(x, x, TN, preferred_element_type=jnp.float32)
    sums = jnp.dot(hot, x, preferred_element_type=jnp.float32)
    counts = lax.dot_general(
        jnp.ones((8, seg), jnp.bfloat16), hot, NT, preferred_element_type=jnp.float32
    )
    row, col = iota((half, half), 0), iota((half, half), 1)
    low = moment[half:, half:]
    packed = jnp.where(row >= col, moment[:half, :half], low)
    diag = jnp.sum(jnp.where(row == col, low, 0.0), axis=0, keepdims=True)
    out_ref[q, 0:half, 0:half] = packed
    out_ref[q, 0:half, half:feat] = moment[:half, half:]
    out_ref[q, half : half + CLASSES, :] = sums
    top = half + CLASSES
    out_ref[q, top : top + 8, 0:half] = jnp.concatenate(
        [counts, jnp.zeros((8, half - CLASSES), jnp.float32)], axis=1
    )
    out_ref[q, top : top + 8, half:feat] = jnp.broadcast_to(diag, (8, half))


def reduce_kernel(
    n,
    owners_hbm,
    x_hbm,
    ids_hbm,
    labels_hbm,
    out_ref,
    owners_ref,
    x_ref,
    ids_ref,
    labels_ref,
    acc,
    landed,
    load_sems,
    send_sems,
    recv_sems,
):
    bits = n.bit_length() - 1
    me = lax.axis_index("rows")
    barrier = pltpu.get_barrier_semaphore()
    pairs = [(owners_hbm, owners_ref), (ids_hbm, ids_ref), (labels_hbm, labels_ref), (x_hbm, x_ref)]
    loads = [pltpu.make_async_copy(a, b, load_sems.at[k]) for k, (a, b) in enumerate(pairs)]
    for load in loads:
        load.start()
    for bit in range(bits):
        pl.semaphore_signal(barrier, inc=1, device_id={"rows": partner_of(me, bit)})
    for load in loads:
        load.wait()
    pl.semaphore_wait(barrier, bits)

    def copy_of(step, q):
        return pltpu.make_async_remote_copy(
            src_ref=acc.at[q],
            dst_ref=landed.at[q],
            send_sem=send_sems.at[q],
            recv_sem=recv_sems.at[q],
            device_id={"rows": partner_of(me, step)},
        )

    def partial(q):
        slot = 0
        for b in range(bits):
            mine, theirs = (me // (1 << b)) % 2, (q // (1 << (bits - 1 - b))) % 2
            slot = slot + (1 << b) * ((mine + theirs) % 2)
        node = 0
        for k in range(n):
            node = jnp.where(owners_ref[k] == slot, k, node)
        one_partial(node, q, x_ref, ids_ref, labels_ref, acc)

    def finish(q):
        copy_of(0, q + n // 2).wait_recv()
        acc[q] = acc[q] + landed[q + n // 2]

    def pair(i, carry):
        q = n // 2 - 1 - i
        partial(q + n // 2)
        copy_of(0, q + n // 2).start()
        partial(q)

        @pl.when(i >= 1)
        def _():
            finish(q + 1)

            @pl.when(q + 1 >= n // 4)
            def _():
                copy_of(1, q + 1).start()

        return carry

    lax.fori_loop(0, n // 2, pair, 0)
    finish(0)
    for step in range(1, bits):
        half = n >> (step + 1)
        for q in reversed(range(half)):
            copy_of(step, q + half).wait_recv()
            total = acc[q] + landed[q + half]
            if step == bits - 1:
                out_ref[...] = total
            else:
                acc[q] = total
                if q >= half // 2:
                    copy_of(step + 1, q).start()
    for step in range(bits):
        half = n >> (step + 1)
        for q in range(half, 2 * half):
            copy_of(step, q).wait_send()


def lane_of(x, lane):
    return jnp.broadcast_to(x[:, lane : lane + 1], x.shape)


def solve_kernel(sum_ref, planes_ref, message_ref, work):
    half = LANES
    feat = sum_ref.shape[1]
    top = half + CLASSES
    square = sum_ref[0:half, 0:half]
    turned = square.T
    row, col = iota((half, half), 0), iota((half, half), 1)
    diag = sum_ref[top : top + 1, half:feat]
    first = jnp.where(row >= col, square, turned)
    last = jnp.where(row < col, square, jnp.where(row == col, diag, turned))
    cross = sum_ref[0:half, half:feat]
    sums = sum_ref[half:top, :]
    count_row = sum_ref[top : top + 1, 0:CLASSES]
    eye = iota((CLASSES, CLASSES), 0) == iota((CLASSES, CLASSES), 1)
    counts = jnp.sum(jnp.where(eye, count_row, 0.0), axis=1, keepdims=True)
    total = jnp.sum(counts, axis=0, keepdims=True)
    centers = jnp.sum(sums, axis=0, keepdims=True) / total
    scaled = sums / jnp.maximum(counts, 1.0)
    between = lax.dot_general(
        scaled, sums, TN, precision=HIGHEST, preferred_element_type=jnp.float32
    )
    ridge = jnp.where(row == col, RIDGE, 0.0)
    work[0:half, 0:half] = (first - between[:half, :half]) / total + ridge
    work[0:half, half:feat] = (cross - between[:half, half:]) / total
    work[half:feat, 0:half] = (cross.T - between[half:, :half]) / total
    work[half:feat, half:feat] = (last - between[half:, half:]) / total + ridge
    work[feat : feat + CLASSES, :] = (sums - counts * centers) / total

    rows = feat + CLASSES
    lanes = iota((1, LANES), 1)

    def four(group, base, lane, tile, start):
        pivots = work[pl.ds(group, 8), tile * LANES : (tile + 1) * LANES]
        other = work[pl.ds(group, 8), (1 - tile) * LANES : (2 - tile) * LANES]
        spread = [lane_of(pivots, lane + u) for u in range(4)]
        d = [[spread[u][base + t : base + t + 1, :] for u in range(4)] for t in range(4)]
        a, b, c = d[0][0], d[0][1], d[1][1]
        inv = 1.0 / (a * c - b * b)
        p00, p01, p11 = c * inv, -b * inv, a * inv
        q00, q01, q10, q11 = d[0][2], d[0][3], d[1][2], d[1][3]
        t00, t01 = p00 * q00 + p01 * q10, p00 * q01 + p01 * q11
        t10, t11 = p01 * q00 + p11 * q10, p01 * q01 + p11 * q11
        s00 = d[2][2] - (q00 * t00 + q10 * t10)
        s01 = d[2][3] - (q00 * t01 + q10 * t11)
        s11 = d[3][3] - (q01 * t01 + q11 * t11)
        inv = 1.0 / (s00 * s11 - s01 * s01)
        h00, h01, h11 = s11 * inv, -s01 * inv, s00 * inv
        u00, u01 = t00 * h00 + t01 * h01, t00 * h01 + t01 * h11
        u10, u11 = t10 * h00 + t11 * h01, t10 * h01 + t11 * h11
        e00 = p00 + u00 * t00 + u01 * t01
        e01 = p01 + u00 * t10 + u01 * t11
        e11 = p11 + u10 * t10 + u11 * t11
        dinv = [
            [e00, e01, -u00, -u01],
            [e01, e11, -u10, -u11],
            [-u00, -u10, h00, h01],
            [-u01, -u11, h01, h11],
        ]
        inside = (lanes >= lane) & (lanes < lane + 4)
        near = [
            jnp.where(inside, jnp.where(lanes == lane + t, -1.0, 0.0), pivots[base + t : base + t + 1, :])
            for t in range(4)
        ]
        far = [other[base + t : base + t + 1, :] for t in range(4)]
        mix = lambda r, t: (dinv[t][0] * r[0] + dinv[t][1] * r[1]) + (dinv[t][2] * r[2] + dinv[t][3] * r[3])
        wn = [jnp.broadcast_to(mix(near, t), (8, LANES)) for t in range(4)]
        wf = [jnp.broadcast_to(mix(far, t), (8, LANES)) for t in range(4)]
        inside8 = jnp.broadcast_to(inside, (8, LANES))
        for g in range(start, rows, 8):
            x = work[g : g + 8, tile * LANES : (tile + 1) * LANES]
            y = work[g : g + 8, (1 - tile) * LANES : (2 - tile) * LANES]
            k = [lane_of(x, lane + u) for u in range(4)]
            x = jnp.where(inside8, 0.0, x)
            x = x - ((k[0] * wn[0] + k[1] * wn[1]) + (k[2] * wn[2] + k[3] * wn[3]))
            y = y - ((k[0] * wf[0] + k[1] * wf[1]) + (k[2] * wf[2] + k[3] * wf[3]))
            work[g : g + 8, tile * LANES : (tile + 1) * LANES] = x
            work[g : g + 8, (1 - tile) * LANES : (2 - tile) * LANES] = y

    for pivot in range(0, feat, 4):
        group, base = pivot // 8 * 8, pivot % 8
        four(group, base, pivot % LANES, pivot // LANES, group if base == 0 else group + 8)

    planes = work[feat : feat + CLASSES, :]
    planes_ref[...] = planes
    offsets = -jnp.sum(planes * centers, axis=1, keepdims=True)
    high = offsets.astype(jnp.bfloat16).astype(jnp.float32)
    middle = (offsets - high).astype(jnp.bfloat16).astype(jnp.float32)
    low = offsets - high - middle
    lane = iota((CLASSES, feat), 1)
    coded = jnp.where(lane < LANES, high, jnp.where(lane < LANES + LANES // 2, middle, low))
    message_ref[0:CLASSES, :] = planes.astype(jnp.bfloat16)
    message_ref[CLASSES : 2 * CLASSES, :] = coded.astype(jnp.bfloat16)


def gather_kernel(n, mine_ref, out_ref, local_sem, send_sems, recv_sems, on_sems, got_sems):
    me = lax.axis_index("rows")
    near = partner_of(me, 0)
    barrier = pltpu.get_barrier_semaphore()
    for t in range(1, n // 2):
        pl.semaphore_signal(barrier, inc=1, device_id={"rows": lax.rem(me + 2 * t, n)})
    pl.semaphore_signal(barrier, inc=1, device_id={"rows": near})
    own = pltpu.make_async_copy(mine_ref, out_ref.at[me], local_sem)
    own.start()
    pl.semaphore_wait(barrier, n // 2)

    def far_copy(t):
        return pltpu.make_async_remote_copy(
            src_ref=mine_ref,
            dst_ref=out_ref.at[me],
            send_sem=send_sems.at[t],
            recv_sem=recv_sems.at[t],
            device_id={"rows": lax.rem(me + 2 * t, n)},
        )

    def near_copy(t):
        source = lax.rem(me + n - 2 * t, n)
        return pltpu.make_async_remote_copy(
            src_ref=mine_ref if t == 0 else out_ref.at[source],
            dst_ref=out_ref.at[source],
            send_sem=on_sems.at[t],
            recv_sem=got_sems.at[t],
            device_id={"rows": near},
        )

    turns = sorted(range(1, n // 2), key=lambda t: -min(t, n // 2 - t))
    for t in turns:
        far_copy(t).start()
    near_copy(0).start()
    own.wait()
    for t in reversed(turns):
        far_copy(t).wait_recv()
        near_copy(t).start()
    for t in turns:
        far_copy(t).wait_send()
    for t in range(n // 2):
        near_copy(t).wait()


def score_kernel(n, owners_ref, x_ref, ids_ref, message_ref, out_ref):
    seg = x_ref.shape[0] * pl.num_programs(0) // n
    some = x_ref.shape[0] // seg
    pieces = seg // LANES
    quarter = LANES + LANES // 2
    for k in range(some):
        node = pl.program_id(0) * some + k
        block = owners_ref[node]
        planes = message_ref[block, 0:CLASSES, :]
        coded = message_ref[block, CLASSES : 2 * CLASSES, :].astype(jnp.float32)
        offsets = coded[:, 0:1] + coded[:, LANES : LANES + 1] + coded[:, quarter : quarter + 1]
        rows = x_ref[k * seg : (k + 1) * seg, :]
        scores = lax.dot_general(planes, rows, NT, preferred_element_type=jnp.float32)
        scores = scores + offsets
        ids = ids_ref[pl.ds(node * pieces, pieces), :]
        for q in range(pieces):
            part = scores[:, q * LANES : (q + 1) * LANES]
            at = k * seg + q * LANES
            out_ref[:, at : at + LANES] = jnp.where(ids[q : q + 1, :] == node, part, 0.0)


def on_device(features, node_ids, labels, owners):
    row_count, feat = features.shape
    n = owners.shape[0]
    seg = row_count // n
    half = feat // 2
    depth = half + CLASSES + 8
    ids = node_ids.reshape(row_count // LANES, LANES)
    tags = labels.reshape(row_count // LANES, LANES)

    whole = pl.BlockSpec(memory_space=pltpu.VMEM)
    summed = pl.pallas_call(
        functools.partial(reduce_kernel, n),
        out_shape=jax.ShapeDtypeStruct((depth, feat), jnp.float32),
        in_specs=[pl.BlockSpec(memory_space=pltpu.HBM)] * 4,
        out_specs=whole,
        scratch_shapes=[
            pltpu.SMEM((n,), jnp.int32),
            pltpu.VMEM((n, seg, feat), features.dtype),
            pltpu.VMEM(ids.shape, jnp.int32),
            pltpu.VMEM(ids.shape, jnp.int32),
            pltpu.VMEM((n, depth, feat), jnp.float32),
            pltpu.VMEM((n, depth, feat), jnp.float32),
            pltpu.SemaphoreType.DMA((4,)),
            pltpu.SemaphoreType.DMA((n,)),
            pltpu.SemaphoreType.DMA((n,)),
        ],
        compiler_params=pltpu.CompilerParams(
            collective_id=0, has_side_effects=True, vmem_limit_bytes=63 << 20
        ),
        name="halving",
    )(owners, features.reshape(n, seg, feat), ids, tags)

    planes, message = pl.pallas_call(
        solve_kernel,
        out_shape=(
            jax.ShapeDtypeStruct((CLASSES, feat), jnp.float32),
            jax.ShapeDtypeStruct((2 * CLASSES, feat), jnp.bfloat16),
        ),
        in_specs=[whole],
        out_specs=(whole, whole),
        scratch_shapes=[pltpu.VMEM((feat + CLASSES, feat), jnp.float32)],
        name="solve",
    )(summed)

    messages = pl.pallas_call(
        functools.partial(gather_kernel, n),
        out_shape=jax.ShapeDtypeStruct((n, 2 * CLASSES, feat), jnp.bfloat16),
        in_specs=[whole],
        out_specs=whole,
        scratch_shapes=[
            pltpu.SemaphoreType.DMA,
            pltpu.SemaphoreType.DMA((n // 2,)),
            pltpu.SemaphoreType.DMA((n // 2,)),
            pltpu.SemaphoreType.DMA((n // 2,)),
            pltpu.SemaphoreType.DMA((n // 2,)),
        ],
        compiler_params=pltpu.CompilerParams(collective_id=1, has_side_effects=True),
        name="spread",
    )(message)

    some = 4
    scores = pl.pallas_call(
        functools.partial(score_kernel, n),
        grid_spec=pltpu.PrefetchScalarGridSpec(
            num_scalar_prefetch=1,
            grid=(n // some,),
            in_specs=[
                pl.BlockSpec((some * seg, feat), lambda i, owners: (i, 0)),
                whole,
                whole,
            ],
            out_specs=pl.BlockSpec((CLASSES, some * seg), lambda i, owners: (0, i)),
        ),
        out_shape=jax.ShapeDtypeStruct((CLASSES, row_count), jnp.float32),
        name="scores",
    )(owners, features, ids, messages)
    return planes[None], scores


def solution(mesh):
    in_specs = (P(("leaf", "rows"), None), P(("leaf", "rows")), P(("leaf", "rows")), P("leaf"))
    out_specs = (P(("leaf", "rows"), None, None), P(None, ("leaf", "rows")))
    return jax.shard_map(
        on_device, mesh=mesh, in_specs=in_specs, out_specs=out_specs, check_vma=False
    )
```

```python
import functools
import jax
import jax.numpy as jnp
from jax import lax
from jax.experimental import pallas as pl
from jax.experimental.pallas import tpu as pltpu
from jax.sharding import PartitionSpec as P

CLASSES = 16
LANES = 128
RIDGE = 0.1
HIGHEST = lax.Precision.HIGHEST
TN = (((0,), (0,)), ((), ()))
NT = (((1,), (1,)), ((), ()))


def iota(shape, dim):
    return lax.broadcasted_iota(jnp.int32, shape, dim)


def partner_of(me, bit):
    width = 1 << bit
    return me + width * (1 - 2 * ((me // width) % 2))


def one_partial(node, q, x_ref, ids_ref, labels_ref, out_ref):
    seg, feat = x_ref.shape[1:]
    half = feat // 2
    pieces = seg // LANES
    ids = ids_ref[pl.ds(node * pieces, pieces), :]
    tags = labels_ref[pl.ds(node * pieces, pieces), :]
    live = ids == node
    length = jnp.sum(live.astype(jnp.float32), axis=(0, 1), keepdims=True)
    x = x_ref[node]
    position = iota((seg, 1), 0).astype(jnp.float32)
    x = jnp.where(position < length, x, jnp.zeros((), x.dtype))
    tags = jnp.where(live, tags, -1)
    hot = jnp.concatenate(
        [tags[k : k + 1, :] == iota((CLASSES, LANES), 0) for k in range(pieces)], axis=1
    )
    hot = hot.astype(jnp.float32).astype(jnp.bfloat16)
    moment = lax.dot_general(x, x, TN, preferred_element_type=jnp.float32)
    sums = jnp.dot(hot, x, preferred_element_type=jnp.float32)
    counts = lax.dot_general(
        jnp.ones((8, seg), jnp.bfloat16), hot, NT, preferred_element_type=jnp.float32
    )
    row, col = iota((half, half), 0), iota((half, half), 1)
    low = moment[half:, half:]
    packed = jnp.where(row >= col, moment[:half, :half], low)
    diag = jnp.sum(jnp.where(row == col, low, 0.0), axis=0, keepdims=True)
    out_ref[q, 0:half, 0:half] = packed
    out_ref[q, 0:half, half:feat] = moment[:half, half:]
    out_ref[q, half : half + CLASSES, :] = sums
    top = half + CLASSES
    out_ref[q, top : top + 8, 0:half] = jnp.concatenate(
        [counts, jnp.zeros((8, half - CLASSES), jnp.float32)], axis=1
    )
    out_ref[q, top : top + 8, half:feat] = jnp.broadcast_to(diag, (8, half))


def reduce_kernel(
    n,
    owners_hbm,
    x_hbm,
    ids_hbm,
    labels_hbm,
    out_ref,
    owners_ref,
    x_ref,
    ids_ref,
    labels_ref,
    acc,
    landed,
    load_sems,
    send_sems,
    recv_sems,
):
    bits = n.bit_length() - 1
    me = lax.axis_index("rows")
    barrier = pltpu.get_barrier_semaphore()
    pairs = [(owners_hbm, owners_ref), (ids_hbm, ids_ref), (labels_hbm, labels_ref), (x_hbm, x_ref)]
    loads = [pltpu.make_async_copy(a, b, load_sems.at[k]) for k, (a, b) in enumerate(pairs)]
    for load in loads:
        load.start()
    for bit in range(bits):
        pl.semaphore_signal(barrier, inc=1, device_id={"rows": partner_of(me, bit)})
    for load in loads:
        load.wait()
    pl.semaphore_wait(barrier, bits)

    def copy_of(step, q):
        return pltpu.make_async_remote_copy(
            src_ref=acc.at[q],
            dst_ref=landed.at[q],
            send_sem=send_sems.at[q],
            recv_sem=recv_sems.at[q],
            device_id={"rows": partner_of(me, step)},
        )

    def partial(q):
        slot = 0
        for b in range(bits):
            mine, theirs = (me // (1 << b)) % 2, (q // (1 << (bits - 1 - b))) % 2
            slot = slot + (1 << b) * ((mine + theirs) % 2)
        node = 0
        for k in range(n):
            node = jnp.where(owners_ref[k] == slot, k, node)
        one_partial(node, q, x_ref, ids_ref, labels_ref, acc)

    def finish(step, q):
        half = n >> (step + 1)
        copy_of(step, q + half).wait_recv()
        acc[q] = acc[q] + landed[q + half]

    quarter = n // 4

    def turn(i):
        low = quarter - 1 - i % quarter
        for b in range(bits - 2):
            yield (low // (1 << b)) % 2, bits - 3 - b
        yield 1 - i // quarter, bits - 2

    def block_at(i):
        return sum(bit * (1 << place) for bit, place in turn(i))

    def pair(i, carry):
        q = block_at(i)
        partial(q + n // 2)
        copy_of(0, q + n // 2).start()
        partial(q)

        @pl.when(i >= 1)
        def _():
            before = block_at(i - 1)
            finish(0, before)

            @pl.when(i - 1 < quarter)
            def _():
                copy_of(1, before).start()

        @pl.when(i >= quarter + 2)
        def _():
            before = block_at(i - 2)
            finish(1, before)

            @pl.when(before >= n // 8)
            def _():
                copy_of(2, before).start()

        return carry

    lax.fori_loop(0, n // 2, pair, 0)
    finish(0, 0)
    ready = {(0, block_at(i)): i for i in range(n // 2)}
    for step in range(1, bits):
        half = n >> (step + 1)
        for q in range(half):
            ready[step, q] = max(ready[step - 1, q], ready[step - 1, q + half] + 1)
    late = {block_at(n // 2 - 2), block_at(n // 2 - 1)}
    rest = [(step, q) for step, q in ready if step > 1 or (step == 1 and q in late)]
    for step, q in sorted(rest, key=lambda event: (ready[event], event)):
        if step == bits - 1:
            copy_of(step, 1).wait_recv()
            out_ref[...] = acc[0] + landed[1]
        else:
            finish(step, q)
            if q >= n >> (step + 2):
                copy_of(step + 1, q).start()
    for step in range(bits):
        half = n >> (step + 1)
        for q in range(half, 2 * half):
            copy_of(step, q).wait_send()


def lane_of(x, lane):
    return jnp.broadcast_to(x[:, lane : lane + 1], x.shape)


def solve_kernel(sum_ref, planes_ref, message_ref, work):
    half = LANES
    feat = sum_ref.shape[1]
    top = half + CLASSES
    square = sum_ref[0:half, 0:half]
    turned = square.T
    row, col = iota((half, half), 0), iota((half, half), 1)
    diag = sum_ref[top : top + 1, half:feat]
    first = jnp.where(row >= col, square, turned)
    last = jnp.where(row < col, square, jnp.where(row == col, diag, turned))
    cross = sum_ref[0:half, half:feat]
    sums = sum_ref[half:top, :]
    count_row = sum_ref[top : top + 1, 0:CLASSES]
    eye = iota((CLASSES, CLASSES), 0) == iota((CLASSES, CLASSES), 1)
    counts = jnp.sum(jnp.where(eye, count_row, 0.0), axis=1, keepdims=True)
    total = jnp.sum(counts, axis=0, keepdims=True)
    centers = jnp.sum(sums, axis=0, keepdims=True) / total
    scaled = sums / jnp.maximum(counts, 1.0)
    between = lax.dot_general(
        scaled, sums, TN, precision=HIGHEST, preferred_element_type=jnp.float32
    )
    ridge = jnp.where(row == col, RIDGE, 0.0)
    work[0:half, 0:half] = (first - between[:half, :half]) / total + ridge
    work[0:half, half:feat] = (cross - between[:half, half:]) / total
    work[half:feat, 0:half] = (cross.T - between[half:, :half]) / total
    work[half:feat, half:feat] = (last - between[half:, half:]) / total + ridge
    work[feat : feat + CLASSES, :] = (sums - counts * centers) / total

    rows = feat + CLASSES
    lanes = iota((1, LANES), 1)

    def four(group, base, lane, tile, start):
        pivots = work[pl.ds(group, 8), tile * LANES : (tile + 1) * LANES]
        other = work[pl.ds(group, 8), (1 - tile) * LANES : (2 - tile) * LANES]
        spread = [lane_of(pivots, lane + u) for u in range(4)]
        d = [[spread[u][base + t : base + t + 1, :] for u in range(4)] for t in range(4)]
        a, b, c = d[0][0], d[0][1], d[1][1]
        inv = 1.0 / (a * c - b * b)
        p00, p01, p11 = c * inv, -b * inv, a * inv
        q00, q01, q10, q11 = d[0][2], d[0][3], d[1][2], d[1][3]
        t00, t01 = p00 * q00 + p01 * q10, p00 * q01 + p01 * q11
        t10, t11 = p01 * q00 + p11 * q10, p01 * q01 + p11 * q11
        s00 = d[2][2] - (q00 * t00 + q10 * t10)
        s01 = d[2][3] - (q00 * t01 + q10 * t11)
        s11 = d[3][3] - (q01 * t01 + q11 * t11)
        inv = 1.0 / (s00 * s11 - s01 * s01)
        h00, h01, h11 = s11 * inv, -s01 * inv, s00 * inv
        u00, u01 = t00 * h00 + t01 * h01, t00 * h01 + t01 * h11
        u10, u11 = t10 * h00 + t11 * h01, t10 * h01 + t11 * h11
        e00 = p00 + u00 * t00 + u01 * t01
        e01 = p01 + u00 * t10 + u01 * t11
        e11 = p11 + u10 * t10 + u11 * t11
        dinv = [
            [e00, e01, -u00, -u01],
            [e01, e11, -u10, -u11],
            [-u00, -u10, h00, h01],
            [-u01, -u11, h01, h11],
        ]
        inside = (lanes >= lane) & (lanes < lane + 4)
        near = [
            jnp.where(inside, jnp.where(lanes == lane + t, -1.0, 0.0), pivots[base + t : base + t + 1, :])
            for t in range(4)
        ]
        far = [other[base + t : base + t + 1, :] for t in range(4)]
        mix = lambda r, t: (dinv[t][0] * r[0] + dinv[t][1] * r[1]) + (dinv[t][2] * r[2] + dinv[t][3] * r[3])
        wn = [jnp.broadcast_to(mix(near, t), (8, LANES)) for t in range(4)]
        wf = [jnp.broadcast_to(mix(far, t), (8, LANES)) for t in range(4)]
        inside8 = jnp.broadcast_to(inside, (8, LANES))
        for g in range(start, rows, 8):
            x = work[g : g + 8, tile * LANES : (tile + 1) * LANES]
            y = work[g : g + 8, (1 - tile) * LANES : (2 - tile) * LANES]
            k = [lane_of(x, lane + u) for u in range(4)]
            x = jnp.where(inside8, 0.0, x)
            x = x - ((k[0] * wn[0] + k[1] * wn[1]) + (k[2] * wn[2] + k[3] * wn[3]))
            y = y - ((k[0] * wf[0] + k[1] * wf[1]) + (k[2] * wf[2] + k[3] * wf[3]))
            work[g : g + 8, tile * LANES : (tile + 1) * LANES] = x
            work[g : g + 8, (1 - tile) * LANES : (2 - tile) * LANES] = y

    for pivot in range(0, feat, 4):
        group, base = pivot // 8 * 8, pivot % 8
        four(group, base, pivot % LANES, pivot // LANES, group if base == 0 else group + 8)

    planes = work[feat : feat + CLASSES, :]
    planes_ref[...] = planes
    offsets = -jnp.sum(planes * centers, axis=1, keepdims=True)
    high = offsets.astype(jnp.bfloat16).astype(jnp.float32)
    middle = (offsets - high).astype(jnp.bfloat16).astype(jnp.float32)
    low = offsets - high - middle
    lane = iota((CLASSES, feat), 1)
    coded = jnp.where(lane < LANES, high, jnp.where(lane < LANES + LANES // 2, middle, low))
    message_ref[0:CLASSES, :] = planes.astype(jnp.bfloat16)
    message_ref[CLASSES : 2 * CLASSES, :] = coded.astype(jnp.bfloat16)


def gather_kernel(n, mine_ref, out_ref, local_sem, send_sems, recv_sems, on_sems, got_sems):
    me = lax.axis_index("rows")
    near = partner_of(me, 0)
    barrier = pltpu.get_barrier_semaphore()
    for t in range(1, n // 2):
        pl.semaphore_signal(barrier, inc=1, device_id={"rows": lax.rem(me + 2 * t, n)})
    pl.semaphore_signal(barrier, inc=1, device_id={"rows": near})
    own = pltpu.make_async_copy(mine_ref, out_ref.at[me], local_sem)
    own.start()
    pl.semaphore_wait(barrier, n // 2)

    def far_copy(t):
        return pltpu.make_async_remote_copy(
            src_ref=mine_ref,
            dst_ref=out_ref.at[me],
            send_sem=send_sems.at[t],
            recv_sem=recv_sems.at[t],
            device_id={"rows": lax.rem(me + 2 * t, n)},
        )

    def near_copy(t):
        source = lax.rem(me + n - 2 * t, n)
        return pltpu.make_async_remote_copy(
            src_ref=mine_ref if t == 0 else out_ref.at[source],
            dst_ref=out_ref.at[source],
            send_sem=on_sems.at[t],
            recv_sem=got_sems.at[t],
            device_id={"rows": near},
        )

    turns = sorted(range(1, n // 2), key=lambda t: -min(t, n // 2 - t))
    for t in turns:
        far_copy(t).start()
    near_copy(0).start()
    own.wait()
    for t in reversed(turns):
        far_copy(t).wait_recv()
        near_copy(t).start()
    for t in turns:
        far_copy(t).wait_send()
    for t in range(n // 2):
        near_copy(t).wait()


def score_kernel(n, owners_ref, x_ref, ids_ref, message_ref, out_ref):
    seg = x_ref.shape[0] * pl.num_programs(0) // n
    some = x_ref.shape[0] // seg
    pieces = seg // LANES
    quarter = LANES + LANES // 2
    for k in range(some):
        node = pl.program_id(0) * some + k
        block = owners_ref[node]
        planes = message_ref[block, 0:CLASSES, :]
        coded = message_ref[block, CLASSES : 2 * CLASSES, :].astype(jnp.float32)
        offsets = coded[:, 0:1] + coded[:, LANES : LANES + 1] + coded[:, quarter : quarter + 1]
        rows = x_ref[k * seg : (k + 1) * seg, :]
        scores = lax.dot_general(planes, rows, NT, preferred_element_type=jnp.float32)
        scores = scores + offsets
        ids = ids_ref[pl.ds(node * pieces, pieces), :]
        for q in range(pieces):
            part = scores[:, q * LANES : (q + 1) * LANES]
            at = k * seg + q * LANES
            out_ref[:, at : at + LANES] = jnp.where(ids[q : q + 1, :] == node, part, 0.0)


def on_device(features, node_ids, labels, owners):
    row_count, feat = features.shape
    n = owners.shape[0]
    seg = row_count // n
    half = feat // 2
    depth = half + CLASSES + 8
    ids = node_ids.reshape(row_count // LANES, LANES)
    tags = labels.reshape(row_count // LANES, LANES)

    whole = pl.BlockSpec(memory_space=pltpu.VMEM)
    summed = pl.pallas_call(
        functools.partial(reduce_kernel, n),
        out_shape=jax.ShapeDtypeStruct((depth, feat), jnp.float32),
        in_specs=[pl.BlockSpec(memory_space=pltpu.HBM)] * 4,
        out_specs=whole,
        scratch_shapes=[
            pltpu.SMEM((n,), jnp.int32),
            pltpu.VMEM((n, seg, feat), features.dtype),
            pltpu.VMEM(ids.shape, jnp.int32),
            pltpu.VMEM(ids.shape, jnp.int32),
            pltpu.VMEM((n, depth, feat), jnp.float32),
            pltpu.VMEM((n, depth, feat), jnp.float32),
            pltpu.SemaphoreType.DMA((4,)),
            pltpu.SemaphoreType.DMA((n,)),
            pltpu.SemaphoreType.DMA((n,)),
        ],
        compiler_params=pltpu.CompilerParams(
            collective_id=0, has_side_effects=True, vmem_limit_bytes=63 << 20
        ),
        name="halving",
    )(owners, features.reshape(n, seg, feat), ids, tags)

    planes, message = pl.pallas_call(
        solve_kernel,
        out_shape=(
            jax.ShapeDtypeStruct((CLASSES, feat), jnp.float32),
            jax.ShapeDtypeStruct((2 * CLASSES, feat), jnp.bfloat16),
        ),
        in_specs=[whole],
        out_specs=(whole, whole),
        scratch_shapes=[pltpu.VMEM((feat + CLASSES, feat), jnp.float32)],
        name="solve",
    )(summed)

    messages = pl.pallas_call(
        functools.partial(gather_kernel, n),
        out_shape=jax.ShapeDtypeStruct((n, 2 * CLASSES, feat), jnp.bfloat16),
        in_specs=[whole],
        out_specs=whole,
        scratch_shapes=[
            pltpu.SemaphoreType.DMA,
            pltpu.SemaphoreType.DMA((n // 2,)),
            pltpu.SemaphoreType.DMA((n // 2,)),
            pltpu.SemaphoreType.DMA((n // 2,)),
            pltpu.SemaphoreType.DMA((n // 2,)),
        ],
        compiler_params=pltpu.CompilerParams(collective_id=1, has_side_effects=True),
        name="spread",
    )(message)

    some = 4
    scores = pl.pallas_call(
        functools.partial(score_kernel, n),
        grid_spec=pltpu.PrefetchScalarGridSpec(
            num_scalar_prefetch=1,
            grid=(n // some,),
            in_specs=[
                pl.BlockSpec((some * seg, feat), lambda i, owners: (i, 0)),
                whole,
                whole,
            ],
            out_specs=pl.BlockSpec((CLASSES, some * seg), lambda i, owners: (0, i)),
        ),
        out_shape=jax.ShapeDtypeStruct((CLASSES, row_count), jnp.float32),
        name="scores",
    )(owners, features, ids, messages)
    return planes[None], scores


def solution(mesh):
    in_specs = (P(("leaf", "rows"), None), P(("leaf", "rows")), P(("leaf", "rows")), P("leaf"))
    out_specs = (P(("leaf", "rows"), None, None), P(None, ("leaf", "rows")))
    return jax.shard_map(
        on_device, mesh=mesh, in_specs=in_specs, out_specs=out_specs, check_vma=False
    )
```
